32 devices in a mesh: query: 8 (over z, y), store: 4 (over x, core).
Axes of the slice: x: 2, y: 2, z: 4, core: 2. Of those that a mesh axis runs over, the one named last changes fastest.
Arguments:
- in_rows: bfloat16 [8, 16384, 64], P('query', 'store'), may hold values from -6 to 6
- out_rows: bfloat16 [8, 16384, 128], P('query', 'store'), may hold values from -0.625 to 0.625
- row_doc: int32 [8, 16384], P('query', 'store'), may hold values from 0 to 31
- row_pos: int32 [8, 16384], P('query', 'store'), may hold values from 0 to 255
- doc_len: int32 [8, 128], P('query', 'store'), may hold values from 128 to 256
- eig_in: float32 [64], replicated, may hold values from 0.25 to 2
- eig_out: float32 [128], replicated, may hold values from 0.25 to 2
- basis_in: float32 [64, 64], replicated, may hold values from -0.75 to 0.75
- basis_out: float32 [128, 128], replicated, may hold values from -0.5 to 0.5
- train_feats: bfloat16 [8, 768, 8192], P('query', 'store'), may hold values from -0.0625 to 0.0625
Outputs:
- scores: bfloat16 [8, 128, 768], P('query', None, 'store')
The draws below stay inside these ranges and needn't reach their ends.
Inputs may be any that keep to these rules, and one draw needn't show every extreme that they name: On each device the 4096 rows form 8 blocks of 512 rows in order; the rows of block j belong to documents of group j in the same store column, and row_doc names the document among that destination's 32.
All inputs are finite; a program needn't handle non-finite values.
Results may differ from the reference program's by a relative error of at most 0.0049.
Values may be sent and summed in bfloat16 or wider, within the bound.
A program may use at most 64 MiB of HBM per device.

```python
import math
import jax
import jax.numpy as jnp
from jax import lax

DIN = 64
DOUT = 128
FEAT = 8192
DOCS_DEV = 32
RPD = 128
SLAB = 192
ROWS_DEV = 4096
CAP = 512
N_QUERY = 8
N_STORE = 4


def plant(drawn, rng, low, largest):
    extent = drawn.shape
    place = [jax.random.randint(jax.random.fold_in(rng, axis), (), 0, extent[axis]) for axis in range(len(extent))]
    drawn = drawn.at[tuple(place)].set(low)
    longest = extent.index(max(extent))
    place[longest] = (place[longest] + 1) % extent[longest]
    return drawn.at[tuple(place)].set(largest)


def shard_levels(rng, extent, pieces, low, top_value):
    def one(dim, blocks):
        steps = jax.random.uniform(jax.random.fold_in(jax.random.fold_in(rng, 6), dim), (blocks,), jnp.float32, low / len(pieces), top_value / len(pieces))
        return jnp.repeat(jnp.exp(steps), extent[dim] // blocks).reshape((-1,) + (1,) * (len(extent) - dim - 1))

    gain = one(*pieces[0])
    for cut in pieces[1:]:
        gain = gain * one(*cut)
    return gain


def normal_values(own_key, shape, width, limit, cuts=(), held_as=jnp.bfloat16):
    values = jax.random.normal(own_key, shape, jnp.float32) * width
    if len(cuts) > 0:
        values = shard_levels(own_key, shape, cuts, -0.22, 0.18) * values
    return jnp.clip(values, min=-limit, max=limit).astype(held_as)


def setup_inputs(seed: int = 0) -> dict:
    key_list = jax.random.split(jax.random.key(seed), 11)
    in_rows = normal_values(key_list[0], (N_QUERY, N_STORE * ROWS_DEV, DIN), 1.0, 6.0, ((0, 8), (1, 4)))
    out_rows = normal_values(key_list[1], (N_QUERY, N_STORE * ROWS_DEV, DOUT), 0.1, 0.625, ((0, 8), (1, 4)))
    row_doc = plant(jax.random.randint(key_list[2], (N_QUERY, N_STORE * ROWS_DEV), 0, DOCS_DEV), jax.random.fold_in(key_list[2], 1), 0, DOCS_DEV - 1).astype(jnp.int32)
    row_pos = plant(jax.random.randint(key_list[3], (N_QUERY, N_STORE * ROWS_DEV), 0, 2 * RPD), jax.random.fold_in(key_list[3], 1), 0, (2 * RPD) - 1).astype(jnp.int32)
    doc_len = plant(jax.random.randint(key_list[4], (N_QUERY, N_STORE * DOCS_DEV), RPD, 2 * RPD + 1), jax.random.fold_in(key_list[4], 1), RPD, 2 * RPD).astype(jnp.int32)
    eig_in = jnp.clip(jnp.exp(jax.random.uniform(key_list[5], (DIN,), jnp.float32, math.log(0.25), math.log(2.0))), 0.25, 2.0)
    eig_out = jnp.clip(jnp.exp(jax.random.uniform(key_list[6], (DOUT,), jnp.float32, math.log(0.25), math.log(2.0))), 0.25, 2.0)
    basis_in = normal_values(key_list[7], (DIN, DIN), DIN ** -0.5, 0.75, (), jnp.float32)
    basis_out = normal_values(key_list[8], (DOUT, DOUT), DOUT ** -0.5, 0.5, (), jnp.float32)
    train_feats = normal_values(key_list[9], (N_QUERY, N_STORE * SLAB, FEAT), FEAT ** -0.5, 0.0625, ((0, 8), (1, 4)))
    return {"in_rows": in_rows, "out_rows": out_rows, "row_doc": row_doc, "row_pos": row_pos, "doc_len": doc_len, "eig_in": eig_in, "eig_out": eig_out, "basis_in": basis_in, "basis_out": basis_out, "train_feats": train_feats}


damping = 0.1
highest = lax.Precision.HIGHEST


def collect(values, target):
    shaped = values.reshape((N_QUERY, N_STORE, N_QUERY, CAP) + values.shape[2:])
    picked = lax.dynamic_index_in_dim(shaped, target, 2, keepdims=False)
    picked = jnp.swapaxes(picked, 0, 1)
    return picked.reshape((N_STORE, N_QUERY * CAP) + values.shape[2:])


def precondition(gradients, scaling, basis_in, basis_out):
    doc_count = gradients.shape[1] // DIN
    rotated = jnp.dot(basis_out.T, gradients, precision=highest)
    turned = jnp.dot(rotated.reshape(DOUT * doc_count, DIN), basis_in, precision=highest)
    turned = turned.reshape(DOUT, doc_count, DIN) * scaling[:, None, :]
    restored = jnp.dot(basis_out, turned.reshape(DOUT, doc_count * DIN), precision=highest)
    final_map = jnp.dot(restored.reshape(DOUT * doc_count, DIN), basis_in.T, precision=highest)
    final_map = final_map.reshape(DOUT, doc_count, DIN)
    return jnp.transpose(final_map, (1, 0, 2)).reshape(doc_count, DOUT * DIN).astype(jnp.bfloat16)


def reference(in_rows, out_rows, row_doc, row_pos, doc_len, eig_in, eig_out, basis_in, basis_out, train_feats):
    scaling = 1.0 / (eig_out[:, None] * eig_in[None, :] + damping)

    def column_feats(operands):
        inputs_side, grads_side, docs_side, pos_side, lengths = operands
        live_mask = (docs_side[:, None] == jnp.arange(DOCS_DEV, dtype=jnp.int32)[None, :]) & (pos_side[:, None] < lengths[None, :])
        weights = live_mask.astype(jnp.float32)
        spread = (weights[:, :, None] * inputs_side.astype(jnp.float32)[:, None, :]).reshape(inputs_side.shape[0], DOCS_DEV * DIN)
        gradients = jnp.dot(grads_side.astype(jnp.float32).T, spread, precision=highest)
        return precondition(gradients, scaling, basis_in, basis_out)

    def score_group(target):
        inputs_all = collect(in_rows, target)
        grads_all = collect(out_rows, target)
        docs_all = collect(row_doc, target)
        pos_all = collect(row_pos, target)
        lengths = lax.dynamic_index_in_dim(doc_len, target, 0, keepdims=False).reshape(N_STORE, DOCS_DEV)
        features = lax.map(column_feats, (inputs_all, grads_all, docs_all, pos_all, lengths))
        queries = features.reshape(N_STORE * DOCS_DEV, FEAT)
        train_rows = lax.dynamic_index_in_dim(train_feats, target, 0, keepdims=False)
        result = jnp.dot(queries.astype(jnp.float32), train_rows.astype(jnp.float32).T, precision=highest)
        return result.astype(jnp.bfloat16)

    return lax.map(score_group, jnp.arange(N_QUERY, dtype=jnp.int32))
```

```python
import functools

import jax
import jax.numpy as jnp
from jax import lax
from jax.experimental import pallas as pl
from jax.experimental.pallas import tpu as pltpu
from jax.sharding import PartitionSpec as P

damping = 0.1
MESH = pl.DeviceIdType.MESH
f32 = jnp.float32
bf16 = jnp.bfloat16


def halves(x):
    high = x.astype(bf16)
    return high, (x - high.astype(f32)).astype(bf16)


def mm(a, b, ca, cb):
    return lax.dot_general(a, b, (((ca,), (cb,)), ((), ())), preferred_element_type=f32)


def kernel(
    queries, stores, x_ref, g_ref, key_ref, len_ref, eig_in_ref, eig_out_ref, bi_ref, bo_ref,
    train_ref, out_ref,
    x_got, g_got, key_got, train, acc, turn, feats,
    x_send, g_send, key_send, x_recv, g_recv, key_recv, own_sem, train_sem,
    far_send, far_recv, near_send, near_recv,
):
    me = lax.axis_index("query")
    column = lax.axis_index("store")
    chips = stores // 2
    chip, core = column // 2, column % 2
    partner = chip * 2 + (1 - core)
    cap = x_ref.shape[2]
    in_width, out_width = bi_ref.shape[0], bo_ref.shape[0]
    docs = len_ref.shape[1]
    half = docs // 2
    slab = train_ref.shape[0]

    train_copy = pltpu.make_async_copy(train_ref, train, train_sem)
    train_copy.start()

    def own_copies():
        rows = pl.ds(pl.multiple_of(me * cap, cap), cap)
        return (
            pltpu.make_async_copy(x_ref.at[me], x_got.at[0], own_sem.at[0]),
            pltpu.make_async_copy(g_ref.at[rows], g_got.at[0], own_sem.at[1]),
            pltpu.make_async_copy(key_ref.at[me], key_got.at[0], own_sem.at[2]),
        )

    for copy in own_copies():
        copy.start()

    barrier = pltpu.get_barrier_semaphore()

    def greet(m, carry):
        pl.semaphore_signal(
            barrier, inc=1, device_id={"query": (me + m) % queries}, device_id_type=MESH
        )
        return carry

    lax.fori_loop(1, queries, greet, 0)
    for d in range(1, chips):
        pl.semaphore_signal(
            barrier, inc=1, device_id={"store": (chip + d) % chips * 2 + core}, device_id_type=MESH
        )
    pl.semaphore_signal(barrier, inc=1, device_id={"store": partner}, device_id_type=MESH)
    pl.semaphore_wait(barrier, (queries - 1) + (chips - 1) + 1)

    def row_copies(m):
        target = (me + m) % queries
        rows = pl.ds(pl.multiple_of(target * cap, cap), cap)
        there = {"query": target}
        return (
            pltpu.make_async_remote_copy(
                key_ref.at[target], key_got.at[m], key_send.at[m], key_recv.at[m],
                device_id=there, device_id_type=MESH,
            ),
            pltpu.make_async_remote_copy(
                g_ref.at[rows], g_got.at[m], g_send.at[m], g_recv.at[m],
                device_id=there, device_id_type=MESH,
            ),
            pltpu.make_async_remote_copy(
                x_ref.at[target], x_got.at[m], x_send.at[m], x_recv.at[m],
                device_id=there, device_id_type=MESH,
            ),
        )

    middle = queries // 2

    def offset(n):
        return (middle + n) % queries

    def launch(n, carry):
        for copy in row_copies((middle + n) % queries):
            copy.start()
        return carry

    lax.fori_loop(0, middle, launch, 0)
    lax.fori_loop(middle + 1, queries, launch, 0)

    bo_high, bo_low = halves(bo_ref[...])
    first = jnp.concatenate([bo_high, bo_low], axis=1)
    first = jnp.concatenate([first, first], axis=0)
    last = jnp.concatenate(
        [
            jnp.concatenate([bo_high, bo_high], axis=1),
            jnp.concatenate([bo_low, bo_low], axis=1),
        ],
        axis=0,
    )
    bi_high, bi_low = halves(bi_ref[...])
    rotate = jnp.concatenate([bi_high, bi_high, bi_low, bi_low], axis=0)
    bt_high, bt_low = halves(bi_ref[...].T)
    restore = jnp.concatenate([bt_high, bt_high, bt_low, bt_low], axis=0)
    square = (in_width, in_width)
    diagonal = lax.broadcasted_iota(jnp.int32, square, 0) == lax.broadcasted_iota(
        jnp.int32, square, 1
    )
    eig_column = jnp.sum(
        jnp.where(diagonal, jnp.broadcast_to(eig_in_ref[...], square), 0.0), axis=1, keepdims=True
    )
    scaling = 1.0 / (eig_column * eig_out_ref[...] + damping)

    group = 8 * in_width

    def absorb(slot, fresh):
        keys = key_got[slot]
        doc = keys // 256
        place = keys % 256
        limit = jnp.zeros_like(doc)
        for e in range(docs):
            limit = jnp.where(doc == e, len_ref[0, e], limit)
        named = jnp.where(place < limit, doc, -1).astype(f32)
        named = jnp.broadcast_to(named, (16, cap)).astype(bf16)[None]
        inputs = x_got[slot].reshape(in_width // 16, 16, cap)
        grads = g_got[slot]
        for start in range(0, docs, 8):
            parts = []
            for c in range(start, start + 8):
                doc_here = (c % 2) * half + c // 2
                kept = jnp.where(
                    named == jnp.asarray(doc_here, bf16), inputs, jnp.zeros_like(inputs)
                )
                parts.append(kept.reshape(in_width, cap))
            spread = jnp.concatenate(parts, axis=0)
            rows = pl.ds(start * in_width, group)
            added = mm(spread, grads, 1, 0)
            if fresh:
                acc[rows, :] = added
            else:
                acc[rows, :] += added

    for copy in own_copies():
        copy.wait()
    absorb(0, True)

    def arrive(n, carry):
        m = (middle + n) % queries
        for copy in row_copies(m):
            copy.wait_recv()
        absorb(m, False)
        return carry

    lax.fori_loop(0, middle, arrive, 0)
    lax.fori_loop(middle + 1, queries, arrive, 0)

    for start in range(0, docs, 8):
        high, low = halves(acc[pl.ds(start * in_width, group), :])
        both = mm(jnp.concatenate([high, low], axis=1), first, 1, 0)
        rotated = both[:, :out_width] + both[:, out_width:]
        wide = jnp.concatenate(
            [rotated[c * in_width : (c + 1) * in_width] for c in range(8)], axis=1
        )
        high, low = halves(wide)
        turned = mm(rotate, jnp.concatenate([high, low, high, low], axis=0), 0, 0)
        turned = turned * jnp.concatenate([scaling] * 8, axis=1)
        high, low = halves(turned)
        restored = mm(restore, jnp.concatenate([high, low, high, low], axis=0), 0, 0)
        tall = jnp.concatenate(
            [restored[:, c * out_width : (c + 1) * out_width] for c in range(8)], axis=0
        )
        high, low = halves(tall)
        both = mm(last, jnp.concatenate([high, low], axis=1), 1, 1)
        final = both[:out_width] + both[out_width:]
        for a in range(4):
            turn[pl.ds(start // 2 + a, out_width, stride=half), :] = final[
                :, a * 2 * in_width : (a + 1) * 2 * in_width
            ]

    lane = lax.broadcasted_iota(jnp.int32, (half, 128), 1)

    def weave(p, carry):
        even = turn[pl.ds(pl.multiple_of(p * 2 * half, 8), half), :]
        odd = turn[pl.ds(pl.multiple_of(p * 2 * half + half, 8), half), :]
        columns = pl.ds(pl.multiple_of(p * 128, 128), 128)
        upper = jnp.where(lane < in_width, even, pltpu.roll(odd, in_width, 1))
        lower = jnp.where(lane < in_width, pltpu.roll(even, in_width, 1), odd)
        feats[0, pl.ds(0, half), columns] = upper.astype(bf16)
        feats[0, pl.ds(half, half), columns] = lower.astype(bf16)
        return carry

    lax.fori_loop(0, out_width // 2, weave, 0, unroll=8)

    def far_copy(d):
        return pltpu.make_async_remote_copy(
            feats.at[0], feats.at[2 * d], far_send.at[d], far_recv.at[d],
            device_id={"store": (chip + d) % chips * 2 + core}, device_id_type=MESH,
        )

    def near_copy(d):
        return pltpu.make_async_remote_copy(
            feats.at[2 * d], feats.at[2 * d + 1], near_send.at[d], near_recv.at[d],
            device_id={"store": partner}, device_id_type=MESH,
        )

    for d in range(1, chips):
        far_copy(d).start()
    near_copy(0).start()
    train_copy.wait()

    def score(slot, owner):
        result = mm(feats[slot], train[...], 1, 1)
        rows = pl.ds(pl.multiple_of(owner * docs, docs), docs)
        out_ref[rows, :] = result.astype(bf16)

    score(0, column)
    near_copy(0).wait_recv()
    score(1, partner)
    for d in range(1, chips):
        origin = (chip + chips - d) % chips * 2
        far_copy(d).wait_recv()
        near_copy(d).start()
        score(2 * d, origin + core)
        near_copy(d).wait_recv()
        score(2 * d + 1, origin + (1 - core))

    def drain(n, carry):
        for copy in row_copies((middle + n) % queries):
            copy.wait_send()
        return carry

    lax.fori_loop(0, middle, drain, 0)
    lax.fori_loop(middle + 1, queries, drain, 0)
    for d in range(1, chips):
        far_copy(d).wait_send()
    for d in range(chips):
        near_copy(d).wait_send()


def on_device(
    queries, stores,
    in_rows, out_rows, row_doc, row_pos, doc_len, eig_in, eig_out, basis_in, basis_out, train_feats,
):
    row_count, in_width = in_rows.shape[1:]
    out_width = out_rows.shape[2]
    docs = doc_len.shape[1]
    slab, feat = train_feats.shape[1:]
    cap = row_count // queries
    inputs = jnp.swapaxes(in_rows[0].reshape(queries, cap, in_width), 1, 2)
    keys = (row_doc * 256 + row_pos).reshape(queries, 1, cap)
    hbm = pl.BlockSpec(memory_space=pl.ANY)
    vmem = pl.BlockSpec(memory_space=pltpu.VMEM)
    smem = pl.BlockSpec(memory_space=pltpu.SMEM)
    dma = pltpu.SemaphoreType.DMA
    chips = stores // 2
    scores = pl.pallas_call(
        functools.partial(kernel, queries, stores),
        name="attribution",
        out_shape=jax.ShapeDtypeStruct((stores * docs, slab), bf16),
        in_specs=[hbm, hbm, hbm, smem, vmem, vmem, vmem, vmem, hbm],
        out_specs=vmem,
        scratch_shapes=[
            pltpu.VMEM((queries, in_width, cap), bf16),
            pltpu.VMEM((queries, cap, out_width), bf16),
            pltpu.VMEM((queries, 1, cap), jnp.int32),
            pltpu.VMEM((slab, feat), bf16),
            pltpu.VMEM((docs * in_width, out_width), f32),
            pltpu.VMEM((docs * in_width, out_width), f32),
            pltpu.VMEM((stores, docs, feat), bf16),
            dma((queries,)), dma((queries,)), dma((queries,)),
            dma((queries,)), dma((queries,)), dma((queries,)),
            dma((3,)), dma,
            dma((chips,)), dma((chips,)), dma((chips,)), dma((chips,)),
        ],
        compiler_params=pltpu.CompilerParams(
            collective_id=0, has_side_effects=True, vmem_limit_bytes=48 * 1024 * 1024
        ),
    )(
        inputs, out_rows[0], keys, doc_len, eig_in[None], eig_out[None], basis_in, basis_out,
        train_feats[0],
    )
    return scores[None]


def solution(mesh):
    placed = (
        P("query", "store", None),
        P("query", "store", None),
        P("query", "store"),
        P("query", "store"),
        P("query", "store"),
        P(),
        P(),
        P(),
        P(),
        P("query", "store", None),
    )
    return jax.shard_map(
        functools.partial(on_device, mesh.shape["query"], mesh.shape["store"]),
        mesh=mesh, in_specs=placed, out_specs=P("query", None, "store"), check_vma=False,
    )
```

```python
import functools

import jax
import jax.numpy as jnp
from jax import lax
from jax.experimental import pallas as pl
from jax.experimental.pallas import tpu as pltpu
from jax.sharding import PartitionSpec as P

damping = 0.1
MESH = pl.DeviceIdType.MESH
f32 = jnp.float32
bf16 = jnp.bfloat16


def halves(x):
    high = x.astype(bf16)
    return high, (x - high.astype(f32)).astype(bf16)


def mm(a, b, ca, cb):
    return lax.dot_general(a, b, (((ca,), (cb,)), ((), ())), preferred_element_type=f32)


def kernel(
    queries, stores, x_ref, g_ref, doc_ref, pos_ref, len_hbm, eig_in_hbm, eig_out_hbm, bi_hbm, bo_hbm,
    train_ref, out_ref,
    len_ref, eig_in_ref, eig_out_ref, bi_ref, bo_ref, small_sem,
    x_got, g_got, doc_got, pos_got, train, acc, turn, feats,
    x_send, g_send, doc_send, pos_send, x_recv, g_recv, doc_recv, pos_recv, own_sem, train_sem,
    far_send, far_recv, near_send, near_recv,
):
    me = lax.axis_index("query")
    column = lax.axis_index("store")
    chips = stores // 2
    chip, core = column // 2, column % 2
    partner = chip * 2 + (1 - core)
    cap = g_ref.shape[0] // queries
    in_width, out_width = bi_ref.shape[0], bo_ref.shape[0]
    docs = len_ref.shape[1]
    half = docs // 2
    slab = train_ref.shape[0]

    small_copies = [
        pltpu.make_async_copy(there, here, small_sem.at[n])
        for n, (there, here) in enumerate(
            (
                (len_hbm, len_ref),
                (eig_in_hbm, eig_in_ref),
                (eig_out_hbm, eig_out_ref),
                (bi_hbm, bi_ref),
                (bo_hbm, bo_ref),
            )
        )
    ]
    train_copy = pltpu.make_async_copy(train_ref, train, train_sem)
    def own_copies():
        rows = pl.ds(pl.multiple_of(me * cap, cap), cap)
        return (
            pltpu.make_async_copy(x_ref.at[:, rows], x_got.at[0], own_sem.at[0]),
            pltpu.make_async_copy(g_ref.at[rows], g_got.at[0], own_sem.at[1]),
            pltpu.make_async_copy(doc_ref.at[:, rows], doc_got.at[0], own_sem.at[2]),
            pltpu.make_async_copy(pos_ref.at[:, rows], pos_got.at[0], own_sem.at[3]),
        )

    barrier = pltpu.get_barrier_semaphore()

    def greet(m, carry):
        pl.semaphore_signal(
            barrier, inc=1, device_id={"query": (me + m) % queries}, device_id_type=MESH
        )
        return carry

    lax.fori_loop(1, queries, greet, 0)
    for d in range(1, chips):
        pl.semaphore_signal(
            barrier, inc=1, device_id={"store": (chip + d) % chips * 2 + core}, device_id_type=MESH
        )
    pl.semaphore_signal(barrier, inc=1, device_id={"store": partner}, device_id_type=MESH)
    pl.semaphore_wait(barrier, (queries - 1) + (chips - 1) + 1)

    def row_copies(m):
        target = (me + m) % queries
        rows = pl.ds(pl.multiple_of(target * cap, cap), cap)
        there = {"query": target}
        return (
            pltpu.make_async_remote_copy(
                doc_ref.at[:, rows], doc_got.at[m], doc_send.at[m], doc_recv.at[m],
                device_id=there, device_id_type=MESH,
            ),
            pltpu.make_async_remote_copy(
                pos_ref.at[:, rows], pos_got.at[m], pos_send.at[m], pos_recv.at[m],
                device_id=there, device_id_type=MESH,
            ),
            pltpu.make_async_remote_copy(
                g_ref.at[rows], g_got.at[m], g_send.at[m], g_recv.at[m],
                device_id=there, device_id_type=MESH,
            ),
            pltpu.make_async_remote_copy(
                x_ref.at[:, rows], x_got.at[m], x_send.at[m], x_recv.at[m],
                device_id=there, device_id_type=MESH,
            ),
        )

    middle = queries // 2

    def launch(n, carry):
        for copy in row_copies((middle + n) % queries):
            copy.start()
        return carry

    lax.fori_loop(0, middle, launch, 0)
    lax.fori_loop(middle + 1, queries, launch, 0)
    for copy in small_copies:
        copy.start()
    for copy in own_copies():
        copy.start()
    train_copy.start()
    for copy in small_copies:
        copy.wait()

    bo_high, bo_low = halves(bo_ref[...])
    first = jnp.concatenate([bo_high, bo_low], axis=1)
    first = jnp.concatenate([first, first], axis=0)
    last = jnp.concatenate(
        [
            jnp.concatenate([bo_high, bo_high], axis=1),
            jnp.concatenate([bo_low, bo_low], axis=1),
        ],
        axis=0,
    )
    bi_high, bi_low = halves(bi_ref[...])
    rotate = jnp.concatenate([bi_high, bi_high, bi_low, bi_low], axis=0)
    bt_high, bt_low = halves(bi_ref[...].T)
    restore = jnp.concatenate([bt_high, bt_high, bt_low, bt_low], axis=0)
    square = (in_width, in_width)
    diagonal = lax.broadcasted_iota(jnp.int32, square, 0) == lax.broadcasted_iota(
        jnp.int32, square, 1
    )
    eig_column = jnp.sum(
        jnp.where(diagonal, jnp.broadcast_to(eig_in_ref[...], square), 0.0), axis=1, keepdims=True
    )
    scaling = 1.0 / (eig_column * eig_out_ref[...] + damping)

    group = 8 * in_width

    def absorb(slot, fresh):
        doc = doc_got[slot]
        place = pos_got[slot]
        limit = jnp.zeros_like(doc)
        for e in range(docs):
            limit = jnp.where(doc == e, len_ref[0, e], limit)
        named = jnp.where(place < limit, doc, -1).astype(f32)
        named = jnp.broadcast_to(named, (16, cap)).astype(bf16)[None]
        inputs = x_got[slot].reshape(in_width // 16, 16, cap)
        grads = g_got[slot]
        for start in range(0, docs, 8):
            parts = []
            for c in range(start, start + 8):
                doc_here = (c % 2) * half + c // 2
                kept = jnp.where(
                    named == jnp.asarray(doc_here, bf16), inputs, jnp.zeros_like(inputs)
                )
                parts.append(kept.reshape(in_width, cap))
            spread = jnp.concatenate(parts, axis=0)
            rows = pl.ds(start * in_width, group)
            added = mm(spread, grads, 1, 0)
            if fresh:
                acc[rows, :] = added
            else:
                acc[rows, :] += added

    for copy in own_copies():
        copy.wait()
    absorb(0, True)

    def arrive(n, carry):
        m = (middle + n) % queries
        for copy in row_copies(m):
            copy.wait_recv()
        absorb(m, False)
        return carry

    lax.fori_loop(0, middle, arrive, 0)
    lax.fori_loop(middle + 1, queries, arrive, 0)

    for start in range(0, docs, 8):
        high, low = halves(acc[pl.ds(start * in_width, group), :])
        both = mm(jnp.concatenate([high, low], axis=1), first, 1, 0)
        rotated = both[:, :out_width] + both[:, out_width:]
        wide = jnp.concatenate(
            [rotated[c * in_width : (c + 1) * in_width] for c in range(8)], axis=1
        )
        high, low = halves(wide)
        turned = mm(rotate, jnp.concatenate([high, low, high, low], axis=0), 0, 0)
        turned = turned * jnp.concatenate([scaling] * 8, axis=1)
        high, low = halves(turned)
        restored = mm(restore, jnp.concatenate([high, low, high, low], axis=0), 0, 0)
        tall = jnp.concatenate(
            [restored[:, c * out_width : (c + 1) * out_width] for c in range(8)], axis=0
        )
        high, low = halves(tall)
        both = mm(last, jnp.concatenate([high, low], axis=1), 1, 1)
        final = both[:out_width] + both[out_width:]
        for a in range(4):
            turn[pl.ds(start // 2 + a, out_width, stride=half), :] = final[
                :, a * 2 * in_width : (a + 1) * 2 * in_width
            ]

    lane = lax.broadcasted_iota(jnp.int32, (half, 128), 1)

    def weave(p, carry):
        even = turn[pl.ds(pl.multiple_of(p * 2 * half, 8), half), :]
        odd = turn[pl.ds(pl.multiple_of(p * 2 * half + half, 8), half), :]
        columns = pl.ds(pl.multiple_of(p * 128, 128), 128)
        upper = jnp.where(lane < in_width, even, pltpu.roll(odd, in_width, 1))
        lower = jnp.where(lane < in_width, pltpu.roll(even, in_width, 1), odd)
        feats[0, pl.ds(0, half), columns] = upper.astype(bf16)
        feats[0, pl.ds(half, half), columns] = lower.astype(bf16)
        return carry

    lax.fori_loop(0, out_width // 2, weave, 0, unroll=8)

    def far_copy(d):
        return pltpu.make_async_remote_copy(
            feats.at[0], feats.at[2 * d], far_send.at[d], far_recv.at[d],
            device_id={"store": (chip + d) % chips * 2 + core}, device_id_type=MESH,
        )

    def near_copy(d):
        return pltpu.make_async_remote_copy(
            feats.at[2 * d], feats.at[2 * d + 1], near_send.at[d], near_recv.at[d],
            device_id={"store": partner}, device_id_type=MESH,
        )

    for d in range(1, chips):
        far_copy(d).start()
    near_copy(0).start()
    train_copy.wait()

    def score(slot, owner):
        result = mm(feats[slot], train[...], 1, 1)
        rows = pl.ds(pl.multiple_of(owner * docs, docs), docs)
        out_ref[rows, :] = result.astype(bf16)

    score(0, column)
    near_copy(0).wait_recv()
    score(1, partner)
    for d in range(1, chips):
        origin = (chip + chips - d) % chips * 2
        far_copy(d).wait_recv()
        near_copy(d).start()
        score(2 * d, origin + core)
        near_copy(d).wait_recv()
        score(2 * d + 1, origin + (1 - core))

    def drain(n, carry):
        for copy in row_copies((middle + n) % queries):
            copy.wait_send()
        return carry

    lax.fori_loop(0, middle, drain, 0)
    lax.fori_loop(middle + 1, queries, drain, 0)
    for d in range(1, chips):
        far_copy(d).wait_send()
    for d in range(chips):
        near_copy(d).wait_send()


def on_device(
    queries, stores,
    in_rows, out_rows, row_doc, row_pos, doc_len, eig_in, eig_out, basis_in, basis_out, train_feats,
):
    row_count, in_width = in_rows.shape[1:]
    out_width = out_rows.shape[2]
    docs = doc_len.shape[1]
    slab, feat = train_feats.shape[1:]
    cap = row_count // queries
    hbm = pl.BlockSpec(memory_space=pltpu.HBM)
    vmem = pl.BlockSpec(memory_space=pltpu.VMEM)
    dma = pltpu.SemaphoreType.DMA
    chips = stores // 2
    scores = pl.pallas_call(
        functools.partial(kernel, queries, stores),
        name="attribution",
        out_shape=jax.ShapeDtypeStruct((stores * docs, slab), bf16),
        in_specs=[hbm] * 10,
        out_specs=vmem,
        scratch_shapes=[
            pltpu.SMEM((1, docs), jnp.int32),
            pltpu.VMEM((1, in_width), f32),
            pltpu.VMEM((1, out_width), f32),
            pltpu.VMEM((in_width, in_width), f32),
            pltpu.VMEM((out_width, out_width), f32),
            dma((5,)),
            pltpu.VMEM((queries, in_width, cap), bf16),
            pltpu.VMEM((queries, cap, out_width), bf16),
            pltpu.VMEM((queries, 1, cap), jnp.int32),
            pltpu.VMEM((queries, 1, cap), jnp.int32),
            pltpu.VMEM((slab, feat), bf16),
            pltpu.VMEM((docs * in_width, out_width), f32),
            pltpu.VMEM((docs * in_width, out_width), f32),
            pltpu.VMEM((stores, docs, feat), bf16),
            dma((queries,)), dma((queries,)), dma((queries,)), dma((queries,)),
            dma((queries,)), dma((queries,)), dma((queries,)), dma((queries,)),
            dma((4,)), dma,
            dma((chips,)), dma((chips,)), dma((chips,)), dma((chips,)),
        ],
        compiler_params=pltpu.CompilerParams(
            collective_id=0, has_side_effects=True, vmem_limit_bytes=67043328
        ),
    )(
        in_rows[0].T, out_rows[0], row_doc, row_pos, doc_len, eig_in[None], eig_out[None], basis_in, basis_out,
        train_feats[0],
    )
    return scores[None]


def solution(mesh):
    placed = (
        P("query", "store", None),
        P("query", "store", None),
        P("query", "store"),
        P("query", "store"),
        P("query", "store"),
        P(),
        P(),
        P(),
        P(),
        P("query", "store", None),
    )
    return jax.shard_map(
        functools.partial(on_device, mesh.shape["query"], mesh.shape["store"]),
        mesh=mesh, in_specs=placed, out_specs=P("query", None, "store"), check_vma=False,
    )
```

```python
import functools

import jax
import jax.numpy as jnp
from jax import lax
from jax.experimental import pallas as pl
from jax.experimental.pallas import tpu as pltpu
from jax.sharding import PartitionSpec as P

damping = 0.1
MESH = pl.DeviceIdType.MESH
f32 = jnp.float32
bf16 = jnp.bfloat16


def halves(x):
    high = x.astype(bf16)
    return high, (x - high.astype(f32)).astype(bf16)


def mm(a, b, ca, cb):
    return lax.dot_general(a, b, (((ca,), (cb,)), ((), ())), preferred_element_type=f32)


def kernel(
    queries, stores, x_ref, g_ref, doc_ref, pos_ref, len_hbm, eig_in_hbm, eig_out_hbm, bi_hbm, bo_hbm,
    train_ref, out_ref,
    len_ref, eig_in_ref, eig_out_ref, bi_ref, bo_ref, small_sem,
    x_got, g_got, doc_got, pos_got, train, acc, turn, feats,
    x_send, g_send, doc_send, pos_send, x_recv, g_recv, doc_recv, pos_recv, own_sem, train_sem,
    far_send, far_recv, near_send, near_recv,
):
    me = lax.axis_index("query")
    column = lax.axis_index("store")
    chips = stores // 2
    chip, core = column // 2, column % 2
    partner = chip * 2 + (1 - core)
    cap = g_ref.shape[0] // queries
    in_width, out_width = bi_ref.shape[0], bo_ref.shape[0]
    docs = len_ref.shape[1]
    batch = 16
    batches = docs // batch
    half = batch // 2
    spans = 2
    span = train_ref.shape[1] // spans

    small_copies = [
        pltpu.make_async_copy(there, here, small_sem.at[n])
        for n, (there, here) in enumerate(
            (
                (len_hbm, len_ref),
                (eig_in_hbm, eig_in_ref),
                (eig_out_hbm, eig_out_ref),
                (bi_hbm, bi_ref),
                (bo_hbm, bo_ref),
            )
        )
    ]
    train_copy = pltpu.make_async_copy(train_ref, train, train_sem)
    def own_copies():
        rows = pl.ds(pl.multiple_of(me * cap, cap), cap)
        return (
            pltpu.make_async_copy(x_ref.at[:, rows], x_got.at[0], own_sem.at[0]),
            pltpu.make_async_copy(g_ref.at[rows], g_got.at[0], own_sem.at[1]),
            pltpu.make_async_copy(doc_ref.at[:, rows], doc_got.at[0], own_sem.at[2]),
            pltpu.make_async_copy(pos_ref.at[:, rows], pos_got.at[0], own_sem.at[3]),
        )

    barrier = pltpu.get_barrier_semaphore()

    def greet(m, carry):
        pl.semaphore_signal(
            barrier, inc=1, device_id={"query": (me + m) % queries}, device_id_type=MESH
        )
        return carry

    lax.fori_loop(1, queries, greet, 0)
    for d in range(1, chips):
        pl.semaphore_signal(
            barrier, inc=1, device_id={"store": (chip + d) % chips * 2 + core}, device_id_type=MESH
        )
    pl.semaphore_signal(barrier, inc=1, device_id={"store": partner}, device_id_type=MESH)
    pl.semaphore_wait(barrier, (queries - 1) + (chips - 1) + 1)

    def row_copies(m):
        target = (me + m) % queries
        rows = pl.ds(pl.multiple_of(target * cap, cap), cap)
        there = {"query": target}
        return (
            pltpu.make_async_remote_copy(
                doc_ref.at[:, rows], doc_got.at[m], doc_send.at[m], doc_recv.at[m],
                device_id=there, device_id_type=MESH,
            ),
            pltpu.make_async_remote_copy(
                pos_ref.at[:, rows], pos_got.at[m], pos_send.at[m], pos_recv.at[m],
                device_id=there, device_id_type=MESH,
            ),
            pltpu.make_async_remote_copy(
                g_ref.at[rows], g_got.at[m], g_send.at[m], g_recv.at[m],
                device_id=there, device_id_type=MESH,
            ),
            pltpu.make_async_remote_copy(
                x_ref.at[:, rows], x_got.at[m], x_send.at[m], x_recv.at[m],
                device_id=there, device_id_type=MESH,
            ),
        )

    middle = queries // 2

    def launch(n, carry):
        for copy in row_copies((middle + n) % queries):
            copy.start()
        return carry

    lax.fori_loop(0, middle, launch, 0)
    lax.fori_loop(middle + 1, queries, launch, 0)
    for copy in small_copies:
        copy.start()
    for copy in own_copies():
        copy.start()
    train_copy.start()
    for copy in small_copies:
        copy.wait()

    bo_high, bo_low = halves(bo_ref[...])
    first = jnp.concatenate([bo_high, bo_low], axis=1)
    first = jnp.concatenate([first, first], axis=0)
    last = jnp.concatenate(
        [
            jnp.concatenate([bo_high, bo_high], axis=1),
            jnp.concatenate([bo_low, bo_low], axis=1),
        ],
        axis=0,
    )
    bi_high, bi_low = halves(bi_ref[...])
    rotate = jnp.concatenate([bi_high, bi_high, bi_low, bi_low], axis=0)
    bt_high, bt_low = halves(bi_ref[...].T)
    restore = jnp.concatenate([bt_high, bt_high, bt_low, bt_low], axis=0)
    square = (in_width, in_width)
    diagonal = lax.broadcasted_iota(jnp.int32, square, 0) == lax.broadcasted_iota(
        jnp.int32, square, 1
    )
    eig_column = jnp.sum(
        jnp.where(diagonal, jnp.broadcast_to(eig_in_ref[...], square), 0.0), axis=1, keepdims=True
    )
    scaling = 1.0 / (eig_column * eig_out_ref[...] + damping)

    group = 8 * in_width

    def absorb(slot, fresh):
        doc = doc_got[slot]
        place = pos_got[slot]
        limit = jnp.zeros_like(doc)
        for e in range(docs):
            limit = jnp.where(doc == e, len_ref[0, e], limit)
        named = jnp.where(place < limit, doc, -1).astype(f32)
        named = jnp.broadcast_to(named, (16, cap)).astype(bf16)[None]
        inputs = x_got[slot].reshape(in_width // 16, 16, cap)
        grads = g_got[slot]
        for start in range(0, docs, 8):
            parts = []
            for c in range(start, start + 8):
                doc_here = c // batch * batch + (c % 2) * half + c % batch // 2
                kept = jnp.where(
                    named == jnp.asarray(doc_here, bf16), inputs, jnp.zeros_like(inputs)
                )
                parts.append(kept.reshape(in_width, cap))
            spread = jnp.concatenate(parts, axis=0)
            rows = pl.ds(start * in_width, group)
            added = mm(spread, grads, 1, 0)
            if fresh:
                acc[rows, :] = added
            else:
                acc[rows, :] += added

    for copy in own_copies():
        copy.wait()
    absorb(0, True)

    def arrive(n, carry):
        m = (middle + n) % queries
        for copy in row_copies(m):
            copy.wait_recv()
        absorb(m, False)
        return carry

    lax.fori_loop(0, middle, arrive, 0)
    lax.fori_loop(middle + 1, queries, arrive, 0)

    def far_copy(d, k, h):
        rows, columns = pl.ds(k * batch, batch), pl.ds(h * span, span)
        return pltpu.make_async_remote_copy(
            feats.at[0, rows, columns], feats.at[2 * d, rows, columns],
            far_send.at[d, k, h], far_recv.at[d, k, h],
            device_id={"store": (chip + d) % chips * 2 + core}, device_id_type=MESH,
        )

    def near_copy(d, k, h):
        rows, columns = pl.ds(k * batch, batch), pl.ds(h * span, span)
        return pltpu.make_async_remote_copy(
            feats.at[2 * d, rows, columns], feats.at[2 * d + 1, rows, columns],
            near_send.at[d, k, h], near_recv.at[d, k, h],
            device_id={"store": partner}, device_id_type=MESH,
        )

    pieces = [(k, h) for k in range(batches) for h in range(spans)]
    lane = lax.broadcasted_iota(jnp.int32, (half, 128), 1)

    def depart(piece):
        for d in range(1, chips):
            far_copy(d, *piece).start()
        near_copy(0, *piece).start()

    def condition(start):
        high, low = halves(acc[pl.ds(start * in_width, group), :])
        both = mm(jnp.concatenate([high, low], axis=1), first, 1, 0)
        rotated = both[:, :out_width] + both[:, out_width:]
        wide = jnp.concatenate(
            [rotated[c * in_width : (c + 1) * in_width] for c in range(8)], axis=1
        )
        high, low = halves(wide)
        turned = mm(rotate, jnp.concatenate([high, low, high, low], axis=0), 0, 0)
        turned = turned * jnp.concatenate([scaling] * 8, axis=1)
        high, low = halves(turned)
        restored = mm(restore, jnp.concatenate([high, low, high, low], axis=0), 0, 0)
        tall = jnp.concatenate(
            [restored[:, c * out_width : (c + 1) * out_width] for c in range(8)], axis=0
        )
        high, low = halves(tall)
        both = mm(last, jnp.concatenate([high, low], axis=1), 1, 1)
        final = both[:out_width] + both[out_width:]
        k, inside = start // batch, start % batch
        for a in range(4):
            turn[k, pl.ds(inside // 2 + a, out_width, stride=half), :] = final[
                :, a * 2 * in_width : (a + 1) * 2 * in_width
            ]

    for n, (k, h) in enumerate(pieces):
        if h == 0:
            for start in range(k * batch, (k + 1) * batch, 8):
                condition(start)

        def weave(p, carry, k=k):
            even = turn[k, pl.ds(pl.multiple_of(p * 2 * half, 8), half), :]
            odd = turn[k, pl.ds(pl.multiple_of(p * 2 * half + half, 8), half), :]
            columns = pl.ds(pl.multiple_of(p * 128, 128), 128)
            upper = jnp.where(lane < in_width, even, pltpu.roll(odd, in_width, 1))
            lower = jnp.where(lane < in_width, pltpu.roll(even, in_width, 1), odd)
            feats[0, pl.ds(k * batch, batch), columns] = jnp.concatenate(
                [upper, lower], axis=0
            ).astype(bf16)
            return carry

        tiles = span // 128
        lax.fori_loop(h * tiles, (h + 1) * tiles, weave, 0, unroll=8)
        if n > 0:
            depart(pieces[n - 1])
    train_copy.wait()
    depart(pieces[-1])

    def put(owner, k, rows, values):
        start = pl.multiple_of(owner * docs + k * batch, batch)
        out_ref[pl.ds(start, rows), :] = values.astype(bf16)

    put(column, 0, docs, mm(feats[0], train[...], 1, 1))
    for piece in pieces:
        near_copy(0, *piece).wait_recv()
    put(partner, 0, docs, mm(feats[1], train[...], 1, 1))

    steps = [(d, k, h) for d in range(1, chips) for k, h in pieces]
    totals = []

    def finish(step):
        d, k, h = step
        near_copy(d, k, h).wait_recv()
        columns = pl.ds(h * span, span)
        queried = feats[2 * d : 2 * d + 2, pl.ds(k * batch, batch), columns]
        part = mm(queried.reshape(2 * batch, span), train[:, columns], 1, 1)
        total = part if h == 0 else totals.pop() + part
        if h < spans - 1:
            totals.append(total)
            return
        origin = (chip + chips - d) % chips * 2
        put(origin + core, k, batch, total[:batch])
        put(origin + (1 - core), k, batch, total[batch:])

    for n, step in enumerate(steps):
        far_copy(*step).wait_recv()
        near_copy(*step).start()
        if n > 0:
            finish(steps[n - 1])
    if steps:
        finish(steps[-1])

    def drain(n, carry):
        for copy in row_copies((middle + n) % queries):
            copy.wait_send()
        return carry

    lax.fori_loop(0, middle, drain, 0)
    lax.fori_loop(middle + 1, queries, drain, 0)
    for piece in pieces:
        for d in range(1, chips):
            far_copy(d, *piece).wait_send()
        for d in range(chips):
            near_copy(d, *piece).wait_send()


def on_device(
    queries, stores,
    in_rows, out_rows, row_doc, row_pos, doc_len, eig_in, eig_out, basis_in, basis_out, train_feats,
):
    row_count, in_width = in_rows.shape[1:]
    out_width = out_rows.shape[2]
    docs = doc_len.shape[1]
    slab, feat = train_feats.shape[1:]
    cap = row_count // queries
    hbm = pl.BlockSpec(memory_space=pltpu.HBM)
    vmem = pl.BlockSpec(memory_space=pltpu.VMEM)
    dma = pltpu.SemaphoreType.DMA
    chips = stores // 2
    scores = pl.pallas_call(
        functools.partial(kernel, queries, stores),
        name="attribution",
        out_shape=jax.ShapeDtypeStruct((stores * docs, slab), bf16),
        in_specs=[hbm] * 10,
        out_specs=vmem,
        scratch_shapes=[
            pltpu.SMEM((1, docs), jnp.int32),
            pltpu.VMEM((1, in_width), f32),
            pltpu.VMEM((1, out_width), f32),
            pltpu.VMEM((in_width, in_width), f32),
            pltpu.VMEM((out_width, out_width), f32),
            dma((5,)),
            pltpu.VMEM((queries, in_width, cap), bf16),
            pltpu.VMEM((queries, cap, out_width), bf16),
            pltpu.VMEM((queries, 1, cap), jnp.int32),
            pltpu.VMEM((queries, 1, cap), jnp.int32),
            pltpu.VMEM((slab, feat), bf16),
            pltpu.VMEM((docs * in_width, out_width), f32),
            pltpu.VMEM((docs // 16, 8 * out_width, 128), f32),
            pltpu.VMEM((stores, docs, feat), bf16),
            dma((queries,)), dma((queries,)), dma((queries,)), dma((queries,)),
            dma((queries,)), dma((queries,)), dma((queries,)), dma((queries,)),
            dma((4,)), dma,
            *[dma((chips, docs // 16, 2))] * 4,
        ],
        compiler_params=pltpu.CompilerParams(
            collective_id=0, has_side_effects=True, vmem_limit_bytes=67043328
        ),
    )(
        in_rows[0].T, out_rows[0], row_doc, row_pos, doc_len, eig_in[None], eig_out[None], basis_in, basis_out,
        train_feats[0],
    )
    return scores[None]


def solution(mesh):
    placed = (
        P("query", "store", None),
        P("query", "store", None),
        P("query", "store"),
        P("query", "store"),
        P("query", "store"),
        P(),
        P(),
        P(),
        P(),
        P("query", "store", None),
    )
    return jax.shard_map(
        functools.partial(on_device, mesh.shape["query"], mesh.shape["store"]),
        mesh=mesh, in_specs=placed, out_specs=P("query", None, "store"), check_vma=False,
    )
```
